32 devices in a mesh: dp: 8 (over z, y), tensor: 4 (over x, core).
Axes of the slice: x: 2, y: 2, z: 4, core: 2. Of those that a mesh axis runs over, the one named last changes fastest.
Arguments:
- hidden_in: bfloat16 [6144, 768], P('dp'), may hold values from -6 to 6
- segment_ids: int32 [8, 768], P('dp'), may hold values from 0 to 3, never falling along the last dimension, each value on 1 to 384 neighbouring positions
- out_grad: bfloat16 [6144, 768], P('dp'), may hold values from -6 to 6
- in_gain: float32 [768], replicated, may hold values from 0.5 to 1.5
- gate_weight: bfloat16 [768, 1536], P(None, 'tensor'), may hold values from -0.21875 to 0.21875
- value_weight: bfloat16 [768, 1536], P(None, 'tensor'), may hold values from -0.21875 to 0.21875
- step_weight: bfloat16 [768, 24], P(None, 'tensor'), may hold values from -0.21875 to 0.21875
- state_weight: bfloat16 [768, 256], replicated, may hold values from -0.21875 to 0.21875
- conv_value_weight: float32 [4, 1536], P(None, 'tensor'), may hold values from -3 to 3
- conv_value_bias: float32 [1536], P('tensor'), may hold values from -3 to 3
- conv_state_weight: float32 [4, 256], replicated, may hold values from -3 to 3
- conv_state_bias: float32 [256], replicated, may hold values from -3 to 3
- step_bias: float32 [24], P('tensor'), may hold values from -6 to -2
- decay_log: float32 [24], P('tensor'), may hold values from -4 to 1
- skip_gain: float32 [24], P('tensor'), may hold values from 0.5 to 1.5
- mix_gain: float32 [1536], P('tensor'), may hold values from 0.5 to 1.5
- out_weight: bfloat16 [1536, 768], P('tensor'), may hold values from -0.15625 to 0.15625
Outputs:
- block_out: float32 [6144, 768], P('dp')
- input_grad: float32 [6144, 768], P('dp')
- grad_in_gain: float32 [768], replicated
- grad_gate_weight: float32 [768, 1536], P(None, 'tensor')
- grad_value_weight: float32 [768, 1536], P(None, 'tensor')
- grad_step_weight: float32 [768, 24], P(None, 'tensor')
- grad_state_weight: float32 [768, 256], replicated
- grad_conv_value_weight: float32 [4, 1536], P(None, 'tensor')
- grad_conv_value_bias: float32 [1536], P('tensor')
- grad_conv_state_weight: float32 [4, 256], replicated
- grad_conv_state_bias: float32 [256], replicated
- grad_step_bias: float32 [24], P('tensor')
- grad_decay_log: float32 [24], P('tensor')
- grad_skip_gain: float32 [24], P('tensor')
- grad_mix_gain: float32 [1536], P('tensor')
- grad_out_weight: float32 [1536, 768], P('tensor')
The draws below stay inside these ranges and needn't reach their ends.
Inputs may be any that keep to these rules, and one draw needn't show every extreme that they name: `segment_ids`: along each sequence segment numbers start at 0 and never fall; each document covers 1 to 384 tokens.
All inputs are finite; a program needn't handle non-finite values.
Results may differ from the reference program's by a relative error of at most 0.012.
The reference program's roundings to bfloat16 on the way (of `normed` and `proj_grad`) count: a program that leaves them out, or rounds other values in their place, can miss the bound.
Values sent between devices are 32-bit elements; how exact they have to be, the bound alone decides.
No kernel may reach another device: no remote copies, remote signals or barrier semaphores. Data moves between devices by JAX's collectives and lax.ppermute only.
A program may use at most 128 MiB of HBM per device.

```python
import math
import jax
import jax.numpy as jnp
import numpy as np
from jax import lax

D = 768
INNER = 1536
HEADS = 24
STATE = 128
KCONV = 4
LEN = 768
SEQS = 8
TOKENS = 6144


def block_levels(stream_key, dims, cuts, low, high):
    level, own = 1.0, jax.random.fold_in(stream_key, 6)
    for dim, blocks in cuts:
        heights = jnp.exp(jax.random.uniform(jax.random.fold_in(own, dim), (blocks,), jnp.float32, low / len(cuts), high / len(cuts)))
        level = level * jnp.repeat(heights, dims[dim] // blocks).reshape([-1 if axis == dim else 1 for axis in range(len(dims))])
    return level


def length_profile(number_of, total, most, slope):
    weights = [(1 << 20) // math.isqrt(grade ** slope) + 1 for grade in range(2, number_of + 1)]
    spare, counts = total - most - (number_of - 1), [1] * (number_of - 1)
    while spare > 0:
        candidates = [i for i in range(number_of - 1) if counts[i] < most]
        mass, left = sum([weights[i] for i in candidates]), spare
        for i in candidates:
            more = min(most - counts[i], max(1, left * weights[i] // mass), spare)
            counts[i] = counts[i] + more
            spare = spare - more
    return np.array([most] + counts)


def ragged(stream_key, number_of, total, bound, lean):
    if number_of == 2:
        one = jax.random.randint(stream_key, (), max(1, total - bound), min(bound, total - 1) + 1)
        return jnp.stack([one, total - one])
    lengths = jnp.asarray(length_profile(number_of, total, bound, lean), jnp.int32)
    pairs = (number_of - 1) // 2
    giver, sink = lengths[1:1 + 2 * pairs:2], lengths[2:2 + 2 * pairs:2]
    room = jnp.minimum(giver - 1, bound - sink)
    passed = jax.random.randint(jax.random.fold_in(stream_key, 1), (pairs,), 0, 1 << 20) % (room + 1)
    lengths = lengths.at[1:1 + 2 * pairs:2].set(giver - passed).at[2:2 + 2 * pairs:2].set(sink + passed)
    return lengths[jax.random.permutation(jax.random.fold_in(stream_key, 2), number_of)]


def noise(own_key, extent, deviation, most, shards=(), held_as=jnp.bfloat16):
    values = deviation * jax.random.normal(own_key, extent, jnp.float32)
    if shards:
        values = values * block_levels(own_key, extent, shards, -0.22, 0.18)
    return jnp.clip(values, -most, most).astype(held_as)


def setup_inputs(seed: int = 0) -> dict:
    streams_of = jax.random.split(jax.random.key(seed), 18)
    hidden_in = noise(streams_of[0], (TOKENS, D), 1.0, 6.0, ((0, 8),))
    segment_ids = jax.vmap(lambda own: jnp.searchsorted(jnp.cumsum(ragged(own, 4, LEN, LEN // 2, 1)), jnp.arange(LEN), side="right"))(jax.random.split(streams_of[1], SEQS)).reshape((SEQS, LEN)).astype(jnp.int32)
    out_grad = noise(streams_of[2], (TOKENS, D), 1.0, 6.0, ((0, 8),))
    in_gain = jnp.clip(1.0 + 0.1 * jax.random.normal(streams_of[3], (D,), jnp.float32), 0.5, 1.5)
    gate_weight = noise(streams_of[4], (D, INNER), D ** -0.5, 0.21875, ((1, 4),))
    value_weight = noise(streams_of[5], (D, INNER), D ** -0.5, 0.21875, ((1, 4),))
    step_weight = noise(streams_of[6], (D, HEADS), D ** -0.5, 0.21875, ((1, 4),))
    state_weight = noise(streams_of[7], (D, 2 * STATE), D ** -0.5, 0.21875)
    conv_value_weight = noise(streams_of[8], (KCONV, INNER), KCONV ** -0.5, 3.0, ((1, 4),), jnp.float32)
    conv_value_bias = noise(streams_of[9], (INNER,), 0.5, 3.0, ((0, 4),), jnp.float32)
    conv_state_weight = noise(streams_of[10], (KCONV, 2 * STATE), KCONV ** -0.5, 3.0, (), jnp.float32)
    conv_state_bias = noise(streams_of[11], (2 * STATE,), 0.5, 3.0, (), jnp.float32)
    step_bias = jnp.clip(-6.0 + 4.0 * jax.random.uniform(streams_of[12], (HEADS,), jnp.float32) ** block_levels(streams_of[12], (HEADS,), ((0, 4),), -0.2, 0.2), -6.0, -2.0)
    decay_log = jnp.clip(-4.0 + 5.0 * jax.random.uniform(streams_of[13], (HEADS,), jnp.float32) ** block_levels(streams_of[13], (HEADS,), ((0, 4),), -0.2, 0.2), -4.0, 1.0)
    skip_gain = jnp.clip(0.5 + 1.0 * jax.random.uniform(streams_of[14], (HEADS,), jnp.float32) ** block_levels(streams_of[14], (HEADS,), ((0, 4),), -0.2, 0.2), 0.5, 1.5)
    mix_gain = jnp.clip(1.0 + 0.1 * jax.random.normal(streams_of[15], (INNER,), jnp.float32), 0.5, 1.5)
    out_weight = noise(streams_of[16], (INNER, D), INNER ** -0.5, 0.15625, ((0, 4),))
    return dict(hidden_in=hidden_in, segment_ids=segment_ids, out_grad=out_grad, in_gain=in_gain, gate_weight=gate_weight, value_weight=value_weight, step_weight=step_weight, state_weight=state_weight, conv_value_weight=conv_value_weight, conv_value_bias=conv_value_bias, conv_state_weight=conv_state_weight, conv_state_bias=conv_state_bias, step_bias=step_bias, decay_log=decay_log, skip_gain=skip_gain, mix_gain=mix_gain, out_weight=out_weight)


EPSILON = 1e-05
HIGHEST = lax.Precision.HIGHEST

def causal_conv(before, taps, offset_bias, segment):
    length = before.shape[0]
    total = offset_bias + taps[0] * before
    for offset in range(1, taps.shape[0]):
        moved = jnp.pad(before, ((offset, 0), (0, 0)))[:length]
        earlier = jnp.pad(segment, (offset, 0), constant_values=-1)[:length]
        keeper = (earlier == segment).astype(jnp.float32)
        total = total + taps[offset] * moved * keeper[:, None]
    return total

def local_mixer(gate_pre, value_pre, state_pre, step_pre, conv_value_weight, conv_value_bias, conv_state_weight, conv_state_bias, step_bias, decay_log, skip_gain, segment):
    length = value_pre.shape[0]
    heads = step_pre.shape[1]
    values = jax.nn.silu(causal_conv(value_pre, conv_value_weight, conv_value_bias, segment))
    states = jax.nn.silu(causal_conv(state_pre, conv_state_weight, conv_state_bias, segment))
    half = states.shape[1] // 2
    inputs_b = states[:, :half]
    readout = states[:, half:]
    step = jax.nn.softplus(step_pre + step_bias)
    decay_sum = jnp.cumsum(step * -jnp.exp(decay_log), axis=0)
    places = jnp.arange(length)
    visible = (places[:, None] >= places[None, :]) & (segment[:, None] == segment[None, :])
    intersection = jnp.dot(readout, inputs_b.T, precision=HIGHEST)
    spread = decay_sum.T[:, :, None] - decay_sum.T[:, None, :]
    mixing = jnp.where(visible, jnp.exp(jnp.where(visible, spread, 0.0)), 0.0) * intersection * step.T[:, None, :]
    per_head = values.reshape(length, heads, -1)
    mixed = jnp.einsum('hts,shp->thp', mixing, per_head, precision=HIGHEST) + skip_gain[None, :, None] * per_head
    return mixed.reshape(length, -1) * jax.nn.silu(gate_pre)

def reference(hidden_in, segment_ids, out_grad, in_gain, gate_weight, value_weight, step_weight, state_weight, conv_value_weight, conv_value_bias, conv_state_weight, conv_state_bias, step_bias, decay_log, skip_gain, mix_gain, out_weight):
    blocks_in = hidden_in.reshape(SEQS, LEN, D)
    blocks_grad = out_grad.reshape(SEQS, LEN, D)
    shapes = (in_gain, gate_weight, value_weight, step_weight, state_weight, conv_value_weight, conv_value_bias, conv_state_weight, conv_state_bias, step_bias, decay_log, skip_gain, mix_gain, out_weight)
    start_totals = tuple((jnp.zeros(array.shape, jnp.float32) for array in shapes))

    def one_sequence(totals, item):
        block, segment, block_grad = item
        hidden = block.astype(jnp.float32)
        inv_rms = lax.rsqrt(lax.optimization_barrier(jnp.mean(hidden * hidden, axis=1, keepdims=True)) + EPSILON)
        scaled = hidden * inv_rms
        normed = (scaled * in_gain).astype(jnp.bfloat16)
        gate_pre = jnp.dot(normed, gate_weight, preferred_element_type=jnp.float32)
        value_pre = jnp.dot(normed, value_weight, preferred_element_type=jnp.float32)
        step_pre = jnp.dot(normed, step_weight, preferred_element_type=jnp.float32)
        state_pre = jnp.dot(normed, state_weight, preferred_element_type=jnp.float32)

        def mixer(gate_part, value_part, state_part, step_part, cvw, cvb, csw, csb, sbias, dlog, sgain):
            return local_mixer(gate_part, value_part, state_part, step_part, cvw, cvb, csw, csb, sbias, dlog, sgain, segment)
        gated, pullback = jax.vjp(mixer, gate_pre, value_pre, state_pre, step_pre, conv_value_weight, conv_value_bias, conv_state_weight, conv_state_bias, step_bias, decay_log, skip_gain)
        weighted = (gated * mix_gain).astype(jnp.bfloat16)
        projected = jnp.dot(weighted, out_weight, preferred_element_type=jnp.float32)
        squares = lax.optimization_barrier(jnp.sum(gated * gated, axis=1, keepdims=True))
        out_scale = lax.rsqrt(squares / INNER + EPSILON)
        result = hidden + out_scale * projected
        upstream = block_grad.astype(jnp.float32)
        scale_grad = lax.optimization_barrier(jnp.sum(upstream * projected, axis=1, keepdims=True))
        proj_grad = (upstream * out_scale).astype(jnp.bfloat16)
        weighted_grad = jnp.dot(proj_grad, out_weight.T, preferred_element_type=jnp.float32)
        out_weight_grad = jnp.dot(weighted.T, proj_grad, preferred_element_type=jnp.float32)
        mix_gain_grad = lax.optimization_barrier(jnp.sum(weighted_grad * gated, axis=0))
        gated_grad = weighted_grad * mix_gain - gated * (scale_grad * out_scale * out_scale * out_scale / INNER)
        pulled = pullback(gated_grad)
        gate_back = pulled[0].astype(jnp.bfloat16)
        value_back = pulled[1].astype(jnp.bfloat16)
        state_back = pulled[2].astype(jnp.bfloat16)
        step_back = pulled[3].astype(jnp.bfloat16)
        normed_grad = jnp.dot(gate_back, gate_weight.T, preferred_element_type=jnp.float32) + jnp.dot(value_back, value_weight.T, preferred_element_type=jnp.float32) + jnp.dot(step_back, step_weight.T, preferred_element_type=jnp.float32) + jnp.dot(state_back, state_weight.T, preferred_element_type=jnp.float32)
        in_gain_grad = lax.optimization_barrier(jnp.sum(normed_grad * scaled, axis=0))
        scaled_grad = normed_grad * in_gain
        input_grad = upstream + inv_rms * (scaled_grad - scaled * lax.optimization_barrier(jnp.mean(scaled_grad * scaled, axis=1, keepdims=True)))
        terms = (in_gain_grad, jnp.dot(normed.T, gate_back, preferred_element_type=jnp.float32), jnp.dot(normed.T, value_back, preferred_element_type=jnp.float32), jnp.dot(normed.T, step_back, preferred_element_type=jnp.float32), jnp.dot(normed.T, state_back, preferred_element_type=jnp.float32), pulled[4], pulled[5], pulled[6], pulled[7], pulled[8], pulled[9], pulled[10], mix_gain_grad, out_weight_grad)
        totals = tuple((older + newer for older, newer in zip(totals, terms)))
        return (totals, (result, input_grad))
    totals, outputs = lax.scan(one_sequence, start_totals, (blocks_in, segment_ids, blocks_grad))
    block_out = outputs[0].reshape(TOKENS, D)
    input_grad = outputs[1].reshape(TOKENS, D)
    return (block_out, input_grad, totals[0], totals[1], totals[2], totals[3], totals[4], totals[5], totals[6], totals[7], totals[8], totals[9], totals[10], totals[11], totals[12], totals[13])
```

```python
import functools

import jax
import jax.numpy as jnp
from jax import lax
from jax.sharding import PartitionSpec as P

EPSILON = 1e-05
HIGHEST = lax.Precision.HIGHEST
F32 = jnp.float32
BF16 = jnp.bfloat16


def flip(array, axis, bit):
    size = lax.axis_size(axis)
    return lax.ppermute(array, axis, [(i, i ^ bit) for i in range(size)])


def bits_of(axis):
    size = lax.axis_size(axis)
    return [1 << k for k in range(size.bit_length() - 1)]


def exchange_sum(array, steps):
    for axis, bit in steps:
        array = array + flip(array, axis, bit)
    return array


def halving_sum(array, halved, whole):
    sides = []
    for axis, bit in halved:
        half = array.shape[0] // 2
        upper = (lax.axis_index(axis) & bit) != 0
        low, high = array[:half], array[half:]
        kept = jnp.where(upper, high, low)
        given = jnp.where(upper, low, high)
        array = kept + flip(given, axis, bit)
        sides.append((axis, bit, upper))
    array = exchange_sum(array, whole)
    for axis, bit, upper in reversed(sides):
        other = flip(array, axis, bit)
        array = jnp.concatenate(
            [jnp.where(upper, other, array), jnp.where(upper, array, other)], axis=0
        )
    return array


def dot_f32(left, right, dims, precision=None):
    return lax.dot_general(
        left, right, (dims, ((), ())), preferred_element_type=F32, precision=precision
    )


def round16(array):
    return lax.reduce_precision(array, 8, 7)


def rows_dot(left, right):
    return dot_f32(left, right, ((0,), (0,)))


def cols_dot(left, right):
    return dot_f32(left, right, ((1,), (1,)))


def keepers(segment, count):
    length = segment.shape[0]
    out = []
    for offset in range(1, count):
        earlier = jnp.pad(segment, (offset, 0), constant_values=-1)[:length]
        out.append((earlier == segment).astype(F32)[:, None])
    return out


def conv_forward(before, taps, bias, keep):
    length = before.shape[0]
    total = bias + taps[0] * before
    for offset in range(1, taps.shape[0]):
        moved = jnp.pad(before, ((offset, 0), (0, 0)))[:length]
        total = total + taps[offset] * moved * keep[offset - 1]
    return total


def conv_backward(before, taps, keep, grad):
    length = before.shape[0]
    back = taps[0] * grad
    tap_grads = [jnp.sum(grad * before, axis=0)]
    for offset in range(1, taps.shape[0]):
        kept = grad * keep[offset - 1]
        moved = jnp.pad(before, ((offset, 0), (0, 0)))[:length]
        tap_grads.append(jnp.sum(kept * moved, axis=0))
        back = back + taps[offset] * jnp.pad(kept, ((0, offset), (0, 0)))[offset:]
    return back, jnp.stack(tap_grads), jnp.sum(grad, axis=0)


def local(
    hidden_in,
    segment_ids,
    out_grad,
    in_gain,
    gate_weight,
    value_weight,
    step_weight,
    state_weight,
    conv_value_weight,
    conv_value_bias,
    conv_state_weight,
    conv_state_bias,
    step_bias,
    decay_log,
    skip_gain,
    mix_gain,
    out_weight,
):
    length = hidden_in.shape[0]
    segment = segment_ids[0]
    heads = step_weight.shape[1]
    width = gate_weight.shape[1]
    inner = width * lax.axis_size("tensor")
    state = state_weight.shape[1] // 2
    head = width // heads
    taps = conv_value_weight.shape[0]
    tensor_steps = [("tensor", b) for b in bits_of("tensor")]
    dp_steps = [("dp", b) for b in bits_of("dp")]

    hidden = hidden_in.astype(F32)
    upstream = out_grad.astype(F32)
    inv_rms = lax.rsqrt(jnp.mean(hidden * hidden, axis=1, keepdims=True) + EPSILON)
    scaled = hidden * inv_rms
    normed = (scaled * in_gain).astype(BF16)
    gate_pre = jnp.dot(normed, gate_weight, preferred_element_type=F32)
    value_pre = jnp.dot(normed, value_weight, preferred_element_type=F32)
    step_pre = jnp.dot(normed, step_weight, preferred_element_type=F32)
    state_pre = jnp.dot(normed, state_weight, preferred_element_type=F32)

    keep = keepers(segment, taps)
    value_conv = conv_forward(value_pre, conv_value_weight, conv_value_bias, keep)
    value_sig = jax.nn.sigmoid(value_conv)
    values = value_conv * value_sig
    state_conv = conv_forward(state_pre, conv_state_weight, conv_state_bias, keep)
    state_sig = jax.nn.sigmoid(state_conv)
    states = state_conv * state_sig
    inputs_b, readout = states[:, :state], states[:, state:]
    step_arg = step_pre + step_bias
    step = jax.nn.softplus(step_arg)
    rate = -jnp.exp(decay_log)
    places = jnp.arange(length)
    causal = places[:, None] >= places[None, :]
    lower = causal.astype(F32)
    cum = dot_f32(lower, step * rate, ((1,), (0,)), HIGHEST)
    visible = causal & (segment[:, None] == segment[None, :])
    seen = jnp.where(visible, dot_f32(readout, inputs_b, ((1,), (1,)), HIGHEST), 0.0)
    cum_t = cum.T
    decay = jnp.exp(jnp.minimum(cum_t[:, :, None] - cum_t[:, None, :], 0.0))
    kernel16 = (decay * seen[None]).astype(BF16)

    def spread(per_head):
        return jnp.repeat(per_head, head, axis=1)

    def head_sum(array):
        return jnp.sum(array.reshape(length, heads, head), axis=2)

    stepped = round16(values * spread(step))
    stepped_h = stepped.astype(BF16).reshape(length, heads, head)
    mixed = jnp.einsum("hts,shp->thp", kernel16, stepped_h, preferred_element_type=F32)
    mixed = mixed.reshape(length, width)
    skip = jnp.repeat(skip_gain, head)
    y = mixed + skip * values
    gate_sig = jax.nn.sigmoid(gate_pre)
    gate_act = gate_pre * gate_sig
    gated = y * gate_act
    weighted = (gated * mix_gain).astype(BF16)
    proj_part = jnp.dot(weighted, out_weight, preferred_element_type=F32)
    pair = jnp.stack([jnp.sum(gated * gated, axis=1), jnp.sum(upstream * proj_part, axis=1)])
    squares, scale_grad = exchange_sum(pair, tensor_steps)

    out_scale = lax.rsqrt(squares / inner + EPSILON)[:, None]
    projected = halving_sum(proj_part, tensor_steps[:1], tensor_steps[1:])
    block_out = hidden + out_scale * projected

    proj_grad = (upstream * out_scale).astype(BF16)
    weighted_grad = cols_dot(proj_grad, out_weight)
    out_weight_grad = rows_dot(weighted, proj_grad)
    mix_gain_grad = jnp.sum(weighted_grad * gated, axis=0)
    cubed = scale_grad[:, None] * out_scale * out_scale * out_scale / inner
    gated_grad = weighted_grad * mix_gain - gated * cubed
    gate_back = (gated_grad * y * (gate_sig + gate_act * (1.0 - gate_sig))).astype(BF16)
    gate_weight_grad = rows_dot(normed, gate_back)
    out_weight_sum = halving_sum(out_weight_grad, dp_steps[:2], dp_steps[2:])
    gate_weight_sum = halving_sum(gate_weight_grad, dp_steps[:2], dp_steps[2:])

    dy = gated_grad * gate_act
    dy16 = round16(dy)
    dy_h = dy16.astype(BF16).reshape(length, heads, head)
    pair_grad = jnp.einsum("thp,shp->hts", dy_h, stepped_h, preferred_element_type=F32)
    seen_grad = jnp.where(visible, jnp.sum(pair_grad * decay, axis=0), 0.0)
    states_grad = jnp.concatenate(
        [
            dot_f32(seen_grad, readout, ((0,), (0,)), HIGHEST),
            dot_f32(seen_grad, inputs_b, ((1,), (0,)), HIGHEST),
        ],
        axis=1,
    )
    state_conv_grad = states_grad * (state_sig + states * (1.0 - state_sig))
    state_grad, conv_state_grad, conv_state_bias_grad = conv_backward(
        state_pre, conv_state_weight, keep, state_conv_grad
    )
    state_back = state_grad.astype(BF16)
    state_weight_grad = rows_dot(normed, state_back)
    state_weight_sum = halving_sum(
        state_weight_grad, tensor_steps + dp_steps[:1], dp_steps[1:]
    )

    pulled = jnp.einsum("hts,thp->shp", kernel16, dy_h, preferred_element_type=F32)
    pulled = pulled.reshape(length, width)
    values_grad = pulled * spread(step) + skip * dy
    value_conv_grad = values_grad * (value_sig + values * (1.0 - value_sig))
    value_grad, conv_value_grad, conv_value_bias_grad = conv_backward(
        value_pre, conv_value_weight, keep, value_conv_grad
    )
    value_back = value_grad.astype(BF16)
    value_weight_grad = rows_dot(normed, value_back)
    value_weight_sum = halving_sum(value_weight_grad, dp_steps[:2], dp_steps[2:])

    skip_grad = jnp.sum(dy * values, axis=0).reshape(heads, head).sum(axis=1)
    row_sum = head_sum(dy16 * mixed)
    col_sum = head_sum(stepped * pulled)
    step_direct = head_sum(values * pulled)
    drift = dot_f32(lower, row_sum - col_sum, ((0,), (0,)), HIGHEST)
    step_grad = step_direct + rate * drift
    decay_grad = jnp.sum(drift * step, axis=0) * rate
    step_arg_grad = step_grad * jax.nn.sigmoid(step_arg)
    step_bias_grad = jnp.sum(step_arg_grad, axis=0)
    step_back = step_arg_grad.astype(BF16)
    step_weight_grad = rows_dot(step_back, normed)

    normed_part = (
        cols_dot(gate_back, gate_weight)
        + cols_dot(value_back, value_weight)
        + cols_dot(step_back, step_weight)
        + cols_dot(state_back, state_weight)
    )
    in_gain_part = jnp.sum(normed_part * scaled, axis=0)
    normed_grad = halving_sum(normed_part, tensor_steps[:1], tensor_steps[1:])
    scaled_grad = normed_grad * in_gain
    input_grad = upstream + inv_rms * (
        scaled_grad - scaled * jnp.mean(scaled_grad * scaled, axis=1, keepdims=True)
    )

    tail = jnp.stack([step_bias_grad, decay_grad, skip_grad]).reshape(-1)
    tail = jnp.pad(tail, (0, width - tail.shape[0]))
    owned = jnp.concatenate(
        [
            step_weight_grad.reshape(-1, width),
            conv_value_grad,
            conv_value_bias_grad[None],
            mix_gain_grad[None],
            tail[None],
        ],
        axis=0,
    )
    owned = exchange_sum(owned, dp_steps)
    base = heads * hidden.shape[1] // width
    step_weight_sum = owned[:base].reshape(heads, -1).T
    tail = owned[base + taps + 2]
    shared = jnp.concatenate(
        [in_gain_part.reshape(-1, 2 * state), conv_state_grad, conv_state_bias_grad[None]], axis=0
    )
    shared = exchange_sum(shared, tensor_steps + dp_steps)
    gains = hidden.shape[1] // (2 * state)
    return (
        block_out,
        input_grad,
        shared[:gains].reshape(-1),
        gate_weight_sum,
        value_weight_sum,
        step_weight_sum,
        state_weight_sum,
        owned[base : base + taps],
        owned[base + taps],
        shared[gains : gains + taps],
        shared[gains + taps],
        tail[:heads],
        tail[heads : 2 * heads],
        tail[2 * heads : 3 * heads],
        owned[base + taps + 1],
        out_weight_sum,
    )


def solution(mesh):
    split = P(None, "tensor")
    own = P("tensor")
    return jax.shard_map(
        local,
        mesh=mesh,
        in_specs=(
            P("dp", None),
            P("dp", None),
            P("dp", None),
            P(),
            split,
            split,
            split,
            P(),
            split,
            own,
            P(),
            P(),
            own,
            own,
            own,
            own,
            P("tensor", None),
        ),
        out_specs=(
            P("dp", None),
            P("dp", None),
            P(),
            split,
            split,
            split,
            P(),
            split,
            own,
            P(),
            P(),
            own,
            own,
            own,
            own,
            P("tensor", None),
        ),
        check_vma=False,
    )
```

```python
import functools

import jax
import jax.numpy as jnp
from jax import lax
from jax.experimental import pallas as pl
from jax.experimental.pallas import tpu as pltpu
from jax.sharding import PartitionSpec as P


EPSILON = 1e-05
HIGHEST = lax.Precision.HIGHEST
F32 = jnp.float32
BF16 = jnp.bfloat16
LANES = 128
BLOCK = 128
SHARED = 24


def flip(array, axis, bit):
    size = lax.axis_size(axis)
    return lax.ppermute(array, axis, [(i, i ^ bit) for i in range(size)])


def bits_of(axis):
    size = lax.axis_size(axis)
    return [1 << k for k in range(size.bit_length() - 1)]


def bit_of(axis, bit):
    return (lax.axis_index(axis) & bit) != 0


def exchange_sum(array, steps):
    for axis, bit in steps:
        array = array + flip(array, axis, bit)
    return array


def halving_sum(array, halved, whole):
    for axis, bit in halved:
        half = array.shape[0] // 2
        upper = bit_of(axis, bit)
        low, high = array[:half], array[half:]
        array = jnp.where(upper, high, low) + flip(jnp.where(upper, low, high), axis, bit)
    array = exchange_sum(array, whole)
    for step in reversed(halved):
        array = gather_halves(array, step, 0)
    return array


def gather_halves(array, step, dim):
    axis, bit = step
    other = flip(array, axis, bit)
    upper = bit_of(axis, bit)
    low, high = jnp.where(upper, other, array), jnp.where(upper, array, other)
    return jnp.concatenate([low, high], axis=dim)


def lanes(mask, width):
    count = -(-width // LANES)
    return jnp.concatenate([mask] * count, axis=1)[:, :width] if count > 1 or width % LANES else mask


def moved_down(array, offset):
    return pltpu.roll(array, offset, 0)


def sigmoid(array):
    return 1.0 / (1.0 + jnp.exp(-array))


def keep_masks(seg_row, length, count):
    column = jnp.broadcast_to(seg_row.astype(F32), (LANES, length)).T
    places = lax.broadcasted_iota(jnp.int32, (length, LANES), 0)
    masks = [
        jnp.where((moved_down(column, j) == column) & (places >= j), 1.0, 0.0)
        for j in range(1, count)
    ]
    return column, masks


def conv_rows(before, taps_ref, bias, masks):
    width = before.shape[1]
    total = bias + taps_ref[0:1] * before
    for j, mask in enumerate(masks, 1):
        total = total + taps_ref[j : j + 1] * (moved_down(before, j) * lanes(mask, width))
    return total


def conv_rows_back(before, taps_ref, masks, grad, grads_ref, row):
    length, width = before.shape
    back = taps_ref[0:1] * grad
    grads_ref[row : row + 1, 0:width] = jnp.sum(grad * before, axis=0, keepdims=True)
    for j, mask in enumerate(masks, 1):
        kept = grad * lanes(mask, width)
        product = jnp.sum(kept * moved_down(before, j), axis=0, keepdims=True)
        grads_ref[row + j : row + j + 1, 0:width] = product
        back = back + taps_ref[j : j + 1] * moved_down(kept, length - j)
    row = row + taps_ref.shape[0]
    grads_ref[row : row + 1, 0:width] = jnp.sum(grad, axis=0, keepdims=True)
    return back


def head_vector(ref, heads):
    lane = lax.broadcasted_iota(jnp.int32, (1, LANES), 1)
    row = jnp.zeros((1, LANES), F32)
    for h in range(heads):
        row = jnp.where(lane == h, ref[h], row)
    return row


def softplus(array):
    return jnp.maximum(array, 0.0) + jnp.log1p(jnp.exp(-jnp.abs(array)))


def head_spread(array, heads, head):
    rows = array.shape[0]
    group = LANES // head
    lane = lax.broadcasted_iota(jnp.int32, (rows, LANES), 1)
    parts = []
    for first in range(0, heads, group):
        part = jnp.broadcast_to(array[:, first : first + 1], (rows, LANES))
        for k in range(1, min(group, heads - first)):
            other = jnp.broadcast_to(array[:, first + k : first + k + 1], (rows, LANES))
            part = jnp.where(lane >= k * head, other, part)
        parts.append(part)
    return jnp.concatenate(parts, axis=1)[:, : heads * head]


def head_row(ref, heads, head):
    lane = lax.broadcasted_iota(jnp.int32, (1, heads * head), 1)
    row = jnp.zeros((1, heads * head), F32)
    for h in range(heads):
        row = jnp.where((lane >= h * head) & (lane < (h + 1) * head), ref[h], row)
    return row


def selector(width, head):
    channel = lax.broadcasted_iota(jnp.int32, (width, LANES), 0)
    lane = lax.broadcasted_iota(jnp.int32, (width, LANES), 1)
    return jnp.where((channel >= lane * head) & (channel < (lane + 1) * head), 1.0, 0.0)


def weight_halves(normed_ref, grad, side, kept_ref, given_ref):
    part = normed_ref.shape[1] // 2
    for target, half in ((given_ref, 1 - side), (kept_ref, side)):
        columns = pl.ds(pl.multiple_of(half * part, LANES), part)
        target[...] = lax.dot_general(
            normed_ref[:, columns], grad, (((0,), (0,)), ((), ())), preferred_element_type=F32
        )


def forward_kernel(
    heads,
    side_ref,
    hidden_ref,
    upstream_ref,
    seg_ref,
    in_gain_ref,
    gate_w_ref,
    value_w_ref,
    step_w_ref,
    state_w_ref,
    cvw_ref,
    cvb_ref,
    csw_ref,
    csb_ref,
    step_bias_ref,
    decay_ref,
    skip_ref,
    mix_ref,
    out_w_ref,
    normed_ref,
    gate_ref,
    value_ref,
    state_ref,
    arg_ref,
    cum_ref,
    mixed_ref,
    kept_ref,
    given_ref,
    pair_ref,
    step_w_pad,
    columns,
    rows_ref,
    stepped_ref,
    b_ref,
    weighted_ref,
    proj_rows,
):
    length = hidden_ref.shape[0]
    width = gate_w_ref.shape[1]
    head = width // heads
    half = state_w_ref.shape[1] // 2
    hidden = hidden_ref[...].astype(F32)
    inv_rms = lax.rsqrt(jnp.mean(hidden * hidden, axis=1, keepdims=True) + EPSILON)
    normed = (hidden * inv_rms * in_gain_ref[...]).astype(BF16)
    normed_ref[...] = normed
    step_w_pad[...] = jnp.zeros_like(step_w_pad)
    step_w_pad[:, 0:heads] = step_w_ref[...]
    step_pre = jnp.dot(normed, step_w_pad[...], preferred_element_type=F32)
    step_arg = step_pre + head_vector(step_bias_ref, heads)
    arg_ref[...] = step_arg
    step = softplus(step_arg)
    rate = -jnp.exp(head_vector(decay_ref, heads))
    places = lax.broadcasted_iota(jnp.int32, (length, length), 0)
    others = lax.broadcasted_iota(jnp.int32, (length, length), 1)
    lower = jnp.where(places >= others, 1.0, 0.0)
    cum = jnp.dot(lower, step * rate, preferred_element_type=F32, precision=HIGHEST)
    cum_ref[...] = cum
    rows_ref[...] = cum.T
    for h in range(heads):
        columns[h] = jnp.broadcast_to(cum[:, h : h + 1], (length, LANES))

    column, masks = keep_masks(seg_ref[...], length, cvw_ref.shape[0])
    state_pre = jnp.dot(normed, state_w_ref[...], preferred_element_type=F32)
    state_ref[...] = state_pre
    state_conv = conv_rows(state_pre, csw_ref, csb_ref[...], masks)
    states = state_conv * sigmoid(state_conv)
    b_ref[...] = states
    value_pre = jnp.dot(normed, value_w_ref[...], preferred_element_type=F32)
    value_ref[...] = value_pre
    value_conv = conv_rows(value_pre, cvw_ref, cvb_ref[...], masks)
    values = value_conv * sigmoid(value_conv)
    stepped_ref[...] = (values * head_spread(step, heads, head)).astype(BF16)

    seg_row = seg_ref[...].astype(F32)
    group = LANES // head
    lane = lax.broadcasted_iota(jnp.int32, (1, LANES), 1)
    for first in range(0, length, BLOCK):
        last = first + BLOCK
        seen = lax.dot_general(
            b_ref[first:last, half : 2 * half],
            b_ref[0:last, 0:half],
            (((1,), (1,)), ((), ())),
            preferred_element_type=F32,
            precision=HIGHEST,
        )
        t_at = first + lax.broadcasted_iota(jnp.int32, (BLOCK, last), 0)
        s_at = lax.broadcasted_iota(jnp.int32, (BLOCK, last), 1)
        visible = (t_at >= s_at) & (lanes(column[first:last], last) == seg_row[:, :last])
        seen = jnp.where(visible, seen, 0.0)
        for base in range(0, heads, group):
            low = base * head
            high = min(width, low + LANES)
            total = jnp.zeros((BLOCK, high - low), F32)
            for k in range(min(group, heads - base)):
                h = base + k
                spread = lanes(columns[h, first:last], last) - rows_ref[h : h + 1, 0:last]
                weight = (jnp.exp(jnp.minimum(spread, 0.0)) * seen).astype(BF16)
                side = (lane >= k * head) & (lane < (k + 1) * head)
                chosen = jnp.where(
                    side[:, : high - low], stepped_ref[0:last, low:high], jnp.zeros((), BF16)
                )
                total = total + jnp.dot(weight, chosen, preferred_element_type=F32)
            mixed_ref[first:last, low:high] = total

    gate_pre = jnp.dot(normed, gate_w_ref[...], preferred_element_type=F32)
    gate_ref[...] = gate_pre
    y = mixed_ref[...] + head_row(skip_ref, heads, head) * values
    gated = y * (gate_pre * sigmoid(gate_pre))
    weighted_ref[...] = (gated * mix_ref[...]).astype(BF16)
    squares = jnp.sum(gated * gated, axis=1, keepdims=True)
    for target, side in ((given_ref, 1 - side_ref[0]), (kept_ref, side_ref[0])):
        rows = pl.ds(pl.multiple_of(side * (length // 2), BLOCK), length // 2)
        proj = jnp.dot(weighted_ref[rows, :], out_w_ref[...], preferred_element_type=F32)
        target[...] = proj
        product = jnp.sum(upstream_ref[rows, :].astype(F32) * proj, axis=1, keepdims=True)
        proj_rows[rows, :] = jnp.broadcast_to(product, (length // 2, LANES))
    scale_grad = proj_rows[...]
    which = lax.broadcasted_iota(jnp.int32, (length, LANES), 1)
    both = jnp.where(which == 0, squares, jnp.where(which == 1, scale_grad, 0.0))
    pair_ref[...] = both.T[0:8]


def gate_kernel(
    heads,
    inner,
    side_ref,
    pair_ref,
    upstream_ref,
    normed_ref,
    gate_ref,
    value_ref,
    mixed_ref,
    seg_ref,
    cvw_ref,
    cvb_ref,
    skip_ref,
    mix_ref,
    out_w_ref,
    out_kept_ref,
    out_given_ref,
    gate_kept_ref,
    gate_given_ref,
    gate_back_ref,
    dy_ref,
    mix_grad_ref,
    scale_ref,
    proj_grad_ref,
):
    length = upstream_ref.shape[0]
    width = gate_ref.shape[1]
    head = width // heads
    pair = jnp.concatenate([pair_ref[...]] * (LANES // 8), axis=0).T
    squares, scale_grad = pair[:, 0:1], pair[:, 1:2]
    out_scale = lax.rsqrt(squares / inner + EPSILON)
    scale_ref[...] = jnp.broadcast_to(out_scale, (length, LANES))
    cubed = scale_grad * out_scale * out_scale * out_scale / inner
    proj_grad = (upstream_ref[...].astype(F32) * out_scale).astype(BF16)
    proj_grad_ref[...] = proj_grad
    weighted_grad = lax.dot_general(
        proj_grad, out_w_ref[...], (((1,), (1,)), ((), ())), preferred_element_type=F32
    )
    _, masks = keep_masks(seg_ref[...], length, cvw_ref.shape[0])
    value_conv = conv_rows(value_ref[...], cvw_ref, cvb_ref[...], masks)
    values = value_conv * sigmoid(value_conv)
    y = mixed_ref[...] + head_row(skip_ref, heads, head) * values
    gate_pre = gate_ref[...]
    gate_sig = sigmoid(gate_pre)
    gate_act = gate_pre * gate_sig
    gated = y * gate_act
    weighted = (gated * mix_ref[...]).astype(BF16)
    part = proj_grad.shape[1] // 2
    for target, side in ((out_given_ref, 1 - side_ref[1]), (out_kept_ref, side_ref[1])):
        columns = pl.ds(pl.multiple_of(side * part, LANES), part)
        target[...] = lax.dot_general(
            weighted, proj_grad_ref[:, columns], (((0,), (0,)), ((), ())), preferred_element_type=F32
        )
    mix_grad_ref[...] = jnp.sum(weighted_grad * gated, axis=0, keepdims=True)
    gated_grad = weighted_grad * mix_ref[...] - gated * cubed
    gate_back = (gated_grad * y * (gate_sig + gate_act * (1.0 - gate_sig))).astype(BF16)
    gate_back_ref[...] = gate_back
    weight_halves(normed_ref, gate_back, side_ref[1], gate_kept_ref, gate_given_ref)
    dy_ref[...] = gated_grad * gate_act


def mixer_back_kernel(
    heads,
    side_ref,
    dy_ref,
    normed_ref,
    value_ref,
    state_ref,
    arg_ref,
    cum_ref,
    mixed_ref,
    seg_ref,
    cvw_ref,
    cvb_ref,
    csw_ref,
    csb_ref,
    decay_ref,
    skip_ref,
    mix_grad_ref,
    value_kept_ref,
    value_given_ref,
    state_kept_ref,
    state_given_ref,
    value_back_ref,
    state_back_ref,
    step_back_ref,
    small_ref,
    columns,
    rows_ref,
    stepped_ref,
    dy16_ref,
    st_ref,
    dst_ref,
    pulled_ref,
):
    length, width = value_ref.shape
    head = width // heads
    half = state_ref.shape[1] // 2
    taps = cvw_ref.shape[0]
    cum = cum_ref[...]
    rows_ref[...] = cum.T
    for h in range(heads):
        columns[h] = jnp.broadcast_to(cum[:, h : h + 1], (length, LANES))
    column, masks = keep_masks(seg_ref[...], length, taps)
    state_conv = conv_rows(state_ref[...], csw_ref, csb_ref[...], masks)
    state_sig = sigmoid(state_conv)
    states = state_conv * state_sig
    st_ref[...] = states
    value_conv = conv_rows(value_ref[...], cvw_ref, cvb_ref[...], masks)
    value_sig = sigmoid(value_conv)
    values = value_conv * value_sig
    step_arg = arg_ref[...]
    step = softplus(step_arg)
    step_wide = head_spread(step, heads, head)
    stepped_ref[...] = (values * step_wide).astype(BF16)
    dy = dy_ref[...]
    dy16_ref[...] = dy.astype(BF16)

    seg_row = seg_ref[...].astype(F32)
    group = LANES // head
    lane = lax.broadcasted_iota(jnp.int32, (1, LANES), 1)
    dst_ref[...] = jnp.zeros_like(dst_ref)
    for first in range(0, length, BLOCK):
        last = first + BLOCK
        span = length - first
        seen = lax.dot_general(
            st_ref[first:last, 0:half],
            st_ref[first:length, half : 2 * half],
            (((1,), (1,)), ((), ())),
            preferred_element_type=F32,
            precision=HIGHEST,
        )
        s_at = lax.broadcasted_iota(jnp.int32, (BLOCK, span), 0)
        t_at = lax.broadcasted_iota(jnp.int32, (BLOCK, span), 1)
        visible = (t_at >= s_at) & (lanes(column[first:last], span) == seg_row[:, first:length])
        seen = jnp.where(visible, seen, 0.0)
        seen_grad = jnp.zeros((BLOCK, span), F32)
        for base in range(0, heads, group):
            low = base * head
            high = min(width, low + LANES)
            total = jnp.zeros((BLOCK, high - low), F32)
            for k in range(min(group, heads - base)):
                h = base + k
                spread = rows_ref[h : h + 1, first:length] - lanes(columns[h, first:last], span)
                decay = jnp.exp(jnp.minimum(spread, 0.0))
                weight = (decay * seen).astype(BF16)
                side = ((lane >= k * head) & (lane < (k + 1) * head))[:, : high - low]
                zero = jnp.zeros((), BF16)
                chosen = jnp.where(side, dy16_ref[first:length, low:high], zero)
                total = total + jnp.dot(weight, chosen, preferred_element_type=F32)
                product = lax.dot_general(
                    jnp.where(side, stepped_ref[first:last, low:high], zero),
                    dy16_ref[first:length, low:high],
                    (((1,), (1,)), ((), ())),
                    preferred_element_type=F32,
                )
                seen_grad = seen_grad + product * decay
            pulled_ref[first:last, low:high] = total
        seen_grad = jnp.where(visible, seen_grad, 0.0)
        dst_ref[first:last, 0:half] = jnp.dot(
            seen_grad,
            st_ref[first:length, half : 2 * half],
            preferred_element_type=F32,
            precision=HIGHEST,
        )
        dst_ref[first:length, half : 2 * half] += lax.dot_general(
            seen_grad,
            st_ref[first:last, 0:half],
            (((0,), (0,)), ((), ())),
            preferred_element_type=F32,
            precision=HIGHEST,
        )

    normed = normed_ref[...]
    state_conv_grad = dst_ref[...] * (state_sig + states * (1.0 - state_sig))
    small_ref[...] = jnp.zeros_like(small_ref)
    at = 8
    state_back = conv_rows_back(
        state_ref[...],
        csw_ref,
        masks,
        state_conv_grad,
        small_ref,
        SHARED,
    ).astype(BF16)
    state_back_ref[...] = state_back
    weight_halves(normed_ref, state_back, side_ref[0], state_kept_ref, state_given_ref)
    pulled = pulled_ref[...]
    skip = head_row(skip_ref, heads, head)
    values_grad = pulled * step_wide + skip * dy
    value_conv_grad = values_grad * (value_sig + values * (1.0 - value_sig))
    value_back = conv_rows_back(
        value_ref[...],
        cvw_ref,
        masks,
        value_conv_grad,
        small_ref,
        at,
    ).astype(BF16)
    value_back_ref[...] = value_back
    weight_halves(normed_ref, value_back, side_ref[1], value_kept_ref, value_given_ref)
    at = at + taps + 1
    small_ref[at : at + 1, 0:width] = mix_grad_ref[...]

    pick = selector(width, head)
    stepped = stepped_ref[...].astype(F32)
    flow = dy16_ref[...].astype(F32) * mixed_ref[...] - stepped * pulled
    flow = jnp.dot(flow, pick, preferred_element_type=F32, precision=HIGHEST)
    direct = jnp.dot(values * pulled, pick, preferred_element_type=F32, precision=HIGHEST)
    places = lax.broadcasted_iota(jnp.int32, (length, length), 0)
    others = lax.broadcasted_iota(jnp.int32, (length, length), 1)
    upper = jnp.where(places <= others, 1.0, 0.0)
    drift = jnp.dot(upper, flow, preferred_element_type=F32, precision=HIGHEST)
    rate = -jnp.exp(head_vector(decay_ref, heads))
    arg_grad = (direct + rate * drift) * sigmoid(step_arg)
    bias_grad = jnp.sum(arg_grad, axis=0, keepdims=True)
    decay_grad = jnp.sum(drift * step, axis=0, keepdims=True) * rate
    skip_grad = jnp.sum(
        jnp.sum(dy * values, axis=0, keepdims=True).T * pick, axis=0, keepdims=True
    )
    small_ref[at + 1 : at + 2, 0:LANES] = bias_grad
    small_ref[at + 2 : at + 3, 0:LANES] = decay_grad
    small_ref[at + 3 : at + 4, 0:LANES] = skip_grad
    step_back = arg_grad.astype(BF16)
    step_back_ref[...] = step_back
    small_ref[0:8] = lax.dot_general(
        step_back, normed, (((0,), (0,)), ((), ())), preferred_element_type=F32
    )[0:8]


def input_back_kernel(
    side_ref,
    hidden_ref,
    gate_back_ref,
    value_back_ref,
    step_back_ref,
    state_back_ref,
    gate_w_ref,
    value_w_ref,
    step_w_ref,
    state_w_ref,
    small_ref,
    kept_ref,
    given_ref,
    packed_ref,
    step_w_pad,
):
    length, features = hidden_ref.shape
    step_w_pad[...] = jnp.zeros_like(step_w_pad)
    step_w_pad[:, 0 : step_w_ref.shape[1]] = step_w_ref[...]
    packed_ref[...] = small_ref[...]
    total = jnp.zeros((1, features), F32)
    dims = (((1,), (1,)), ((), ()))
    for target, side in ((given_ref, 1 - side_ref[0]), (kept_ref, side_ref[0])):
        rows = pl.ds(pl.multiple_of(side * (length // 2), BLOCK), length // 2)
        part = (
            lax.dot_general(gate_back_ref[rows, :], gate_w_ref[...], dims, preferred_element_type=F32)
            + lax.dot_general(value_back_ref[rows, :], value_w_ref[...], dims, preferred_element_type=F32)
            + lax.dot_general(step_back_ref[rows, :], step_w_pad[...], dims, preferred_element_type=F32)
            + lax.dot_general(state_back_ref[rows, :], state_w_ref[...], dims, preferred_element_type=F32)
        )
        target[...] = part
        hidden = hidden_ref[rows, :].astype(F32)
        inv_rms = lax.rsqrt(jnp.mean(hidden * hidden, axis=1, keepdims=True) + EPSILON)
        total = total + jnp.sum(part * (hidden * inv_rms), axis=0, keepdims=True)
    packed_ref[packed_ref.shape[0] - 1 : packed_ref.shape[0]] = total


def call(kernel, args, outs, scratch, flops, smem=()):
    specs = [
        pl.BlockSpec(memory_space=pltpu.SMEM if i in smem else pltpu.VMEM) for i in range(len(args))
    ]
    shapes = [jax.ShapeDtypeStruct(shape, dtype) for shape, dtype in outs]
    size = sum(a.size * a.dtype.itemsize for a in list(args) + shapes)
    return pl.pallas_call(
        kernel,
        out_shape=shapes,
        in_specs=specs,
        out_specs=[pl.BlockSpec(memory_space=pltpu.VMEM)] * len(outs),
        scratch_shapes=scratch,
        cost_estimate=pl.CostEstimate(flops=flops, bytes_accessed=size, transcendentals=0),
    )(*args)


def local(
    hidden_in,
    segment_ids,
    out_grad,
    in_gain,
    gate_weight,
    value_weight,
    step_weight,
    state_weight,
    conv_value_weight,
    conv_value_bias,
    conv_state_weight,
    conv_state_bias,
    step_bias,
    decay_log,
    skip_gain,
    mix_gain,
    out_weight,
):
    length, features = hidden_in.shape
    assert segment_ids.shape == (1, length)
    heads = step_weight.shape[1]
    width = gate_weight.shape[1]
    inner = width * lax.axis_size("tensor")
    both = state_weight.shape[1]
    taps = conv_value_weight.shape[0]
    tensor_steps = [("tensor", b) for b in bits_of("tensor")]
    dp_steps = [("dp", b) for b in bits_of("dp")]
    half, part = length // 2, features // 2
    core, row = bit_of(*tensor_steps[0]), bit_of(*dp_steps[0])
    side = jnp.stack([core, row]).astype(jnp.int32)
    cvb = conv_value_bias[None]
    csb = conv_state_bias[None]
    mix = mix_gain[None]
    gain = in_gain[None]

    normed, gate_pre, value_pre, state_pre, step_arg, cum, mixed, proj_kept, proj_given, pair = call(
        functools.partial(forward_kernel, heads),
        (
            side,
            hidden_in,
            out_grad,
            segment_ids,
            gain,
            gate_weight,
            value_weight,
            step_weight,
            state_weight,
            conv_value_weight,
            cvb,
            conv_state_weight,
            csb,
            step_bias,
            decay_log,
            skip_gain,
            mix,
            out_weight,
        ),
        [
            ((length, features), BF16),
            ((length, width), F32),
            ((length, width), F32),
            ((length, both), F32),
            ((length, LANES), F32),
            ((length, LANES), F32),
            ((length, width), F32),
            ((half, features), F32),
            ((half, features), F32),
            ((8, length), F32),
        ],
        [
            pltpu.VMEM((features, LANES), BF16),
            pltpu.VMEM((heads, length, LANES), F32),
            pltpu.VMEM((LANES, length), F32),
            pltpu.VMEM((length, width), BF16),
            pltpu.VMEM((length, both), F32),
            pltpu.VMEM((length, width), BF16),
            pltpu.VMEM((length, LANES), F32),
        ],
        10 * 2**30,
        (0, 13, 14, 15),
    )
    pair = exchange_sum(pair, tensor_steps)

    (
        out_kept,
        out_given,
        gate_kept,
        gate_given,
        gate_back,
        dy,
        mix_grad,
        out_scale,
    ) = call(
        functools.partial(gate_kernel, heads, inner),
        (
            side,
            pair,
            out_grad,
            normed,
            gate_pre,
            value_pre,
            mixed,
            segment_ids,
            conv_value_weight,
            cvb,
            skip_gain,
            mix,
            out_weight,
        ),
        [
            ((width, part), F32),
            ((width, part), F32),
            ((part, width), F32),
            ((part, width), F32),
            ((length, width), BF16),
            ((length, width), F32),
            ((1, width), F32),
            ((length, LANES), F32),
        ],
        [pltpu.VMEM((length, features), BF16)],
        3 * 2**30,
        (0, 10),
    )

    def dp_sum(kept, given, dim):
        mine = kept + flip(given, *dp_steps[0])
        mine = halving_sum(mine, dp_steps[1:2], dp_steps[2:])
        return gather_halves(mine, dp_steps[0], dim)

    out_weight_sum = dp_sum(out_kept, out_given, 1)
    gate_weight_sum = dp_sum(gate_kept, gate_given, 0)

    hidden = hidden_in.astype(F32)
    upstream = out_grad.astype(F32)

    def my_half(array):
        return jnp.where(core, array[half:], array[:half])

    projected = proj_kept + flip(proj_given, *tensor_steps[0])
    projected = exchange_sum(projected, tensor_steps[1:])
    block_out = my_half(hidden) + my_half(out_scale)[:, :1] * projected
    block_out = gather_halves(block_out, tensor_steps[0], 0)

    (
        value_kept,
        value_given,
        state_kept,
        state_given,
        value_back,
        state_back,
        step_back,
        small,
    ) = call(
        functools.partial(mixer_back_kernel, heads),
        (
            side,
            dy,
            normed,
            value_pre,
            state_pre,
            step_arg,
            cum,
            mixed,
            segment_ids,
            conv_value_weight,
            cvb,
            conv_state_weight,
            csb,
            decay_log,
            skip_gain,
            mix_grad,
        ),
        [
            ((part, width), F32),
            ((part, width), F32),
            ((part, both), F32),
            ((part, both), F32),
            ((length, width), BF16),
            ((length, both), BF16),
            ((length, LANES), BF16),
            ((SHARED + 8, features), F32),
        ],
        [
            pltpu.VMEM((heads, length, LANES), F32),
            pltpu.VMEM((LANES, length), F32),
            pltpu.VMEM((length, width), BF16),
            pltpu.VMEM((length, width), BF16),
            pltpu.VMEM((length, both), F32),
            pltpu.VMEM((length, both), F32),
            pltpu.VMEM((length, width), F32),
        ],
        10 * 2**30,
        (0, 13, 14),
    )
    value_weight_sum = dp_sum(value_kept, value_given, 0)
    state_mine = state_kept + flip(state_given, *tensor_steps[0])
    state_mine = halving_sum(state_mine, tensor_steps[1:] + dp_steps[:1], dp_steps[1:])
    state_weight_sum = gather_halves(state_mine, tensor_steps[0], 0)

    normed_kept, normed_given, small = call(
        input_back_kernel,
        (
            side,
            hidden_in,
            gate_back,
            value_back,
            step_back,
            state_back,
            gate_weight,
            value_weight,
            step_weight,
            state_weight,
            small,
        ),
        [((half, features), F32), ((half, features), F32), ((SHARED + 8, features), F32)],
        [pltpu.VMEM((features, LANES), BF16)],
        2 * 2**30,
        (0,),
    )
    normed_grad = normed_kept + flip(normed_given, *tensor_steps[0])
    normed_grad = exchange_sum(normed_grad, tensor_steps[1:])
    own = my_half(hidden)
    inv_rms = lax.rsqrt(jnp.mean(own * own, axis=1, keepdims=True) + EPSILON)
    scaled = own * inv_rms
    scaled_grad = normed_grad * in_gain
    input_grad = my_half(upstream) + inv_rms * (
        scaled_grad - scaled * jnp.mean(scaled_grad * scaled, axis=1, keepdims=True)
    )
    input_grad = gather_halves(input_grad, tensor_steps[0], 0)

    small = exchange_sum(small, dp_steps)
    shared = exchange_sum(small[SHARED:], tensor_steps)
    at = 8 + taps
    return (
        block_out,
        input_grad,
        shared[7],
        gate_weight_sum,
        value_weight_sum,
        small[:heads].T,
        state_weight_sum,
        small[8:at, :width],
        small[at, :width],
        shared[:taps, :both],
        shared[taps, :both],
        small[at + 2, :heads],
        small[at + 3, :heads],
        small[at + 4, :heads],
        small[at + 1, :width],
        out_weight_sum,
    )


def solution(mesh):
    split = P(None, "tensor")
    own = P("tensor")
    return jax.shard_map(
        local,
        mesh=mesh,
        in_specs=(
            P("dp", None),
            P("dp", None),
            P("dp", None),
            P(),
            split,
            split,
            split,
            P(),
            split,
            own,
            P(),
            P(),
            own,
            own,
            own,
            own,
            P("tensor", None),
        ),
        out_specs=(
            P("dp", None),
            P("dp", None),
            P(),
            split,
            split,
            split,
            P(),
            split,
            own,
            P(),
            P(),
            own,
            own,
            own,
            own,
            P("tensor", None),
        ),
        check_vma=False,
    )
```
